1024 devices in a mesh: dp: 8 (over y, core), expert: 32 (over x, z_lo), hid: 4 (over z_hi).
Axes of the slice: x: 4, y: 4, z: 32 (z_hi: 4, z_lo: 8; z = z_hi * 8 + z_lo), core: 2. Of those that a mesh axis runs over, the one named last changes fastest.
Arguments:
- images_in: bfloat16 [1024, 256, 1024], P(('dp', 'expert', 'hid')), may hold values from -16 to 16
- slot_keys: bfloat16 [1024, 128], replicated, may hold values from -6 to 6
- w_in: bfloat16 [64, 1024, 4096], P('expert', None, 'hid'), may hold values from -0.1875 to 0.1875
- w_out: bfloat16 [64, 4096, 1024], P('expert', 'hid'), may hold values from -0.09375 to 0.09375
Outputs:
- mixed: bfloat16 [1024, 256, 1024], P(('dp', 'expert', 'hid'))
The draws below stay inside these ranges and needn't reach their ends.
All inputs are finite; a program needn't handle non-finite values.
Results may differ from the reference program's by a relative error of at most 0.013.
Values may be sent and summed in bfloat16 or wider, within the bound.
No kernel may reach another device: no remote copies, remote signals or barrier semaphores. Data moves between devices by JAX's collectives and lax.ppermute only.
A program may use at most 32 MiB of HBM per device.

```python
import jax
import jax.numpy as jnp
from jax import lax

D = 1024
FF = 4096
SLOTS = 2
TOK = 256
EXPERTS = 64
IMAGES = 1024
N_HID = 4


def block_levels(stream_key, extent, cuts, smallest, top_value):
    def one(position, blocks):
        draws = jax.random.uniform(jax.random.fold_in(jax.random.fold_in(stream_key, 6), position), (blocks,), jnp.float32, smallest / len(cuts), top_value / len(cuts))
        return jnp.repeat(jnp.exp(draws), extent[position] // blocks).reshape((-1,) + (1,) * (len(extent) - position - 1))

    level = one(*cuts[0])
    for cut in cuts[1:]:
        level = level * one(*cut)
    return level


def gaussian(rng, extent, spread, reach, shards=(), kind=jnp.bfloat16):
    drawn = spread * jax.random.normal(rng, extent, jnp.float32)
    if shards:
        drawn = drawn * block_levels(rng, extent, shards, -0.22, 0.18)
    return jnp.clip(drawn, -reach, reach).astype(kind)


def setup_inputs(seed: int = 0) -> dict:
    key_of = jax.random.split(jax.random.key(seed), 5)
    images_in = gaussian(key_of[0], (IMAGES, TOK, D), 3.0, 16.0, ((0, 1024),))
    slot_keys = gaussian(key_of[1], (D, EXPERTS * SLOTS), 1.0, 6.0)
    w_in = gaussian(key_of[2], (EXPERTS, D, FF), D ** -0.5, 0.1875, ((0, 32), (2, 4)))
    w_out = gaussian(key_of[3], (EXPERTS, FF, D), FF ** -0.5, 0.09375, ((0, 32), (1, 4)))
    return dict(images_in=images_in, slot_keys=slot_keys, w_in=w_in, w_out=w_out)


def normal_rows(values):
    floats = values.astype(jnp.float32)
    return (floats * lax.rsqrt(lax.optimization_barrier(jnp.mean(floats * floats, axis=-1, keepdims=True)) + 1e-06)).astype(jnp.bfloat16)

def unit_columns(values):
    floats = values.astype(jnp.float32)
    return (floats * lax.rsqrt(lax.optimization_barrier(jnp.sum(floats * floats, axis=0, keepdims=True)) + 1e-06)).astype(jnp.bfloat16)

def reference(images_in, slot_keys, w_in, w_out):
    unit_keys = unit_columns(slot_keys)

    def mix_image(tokens):
        normed = normal_rows(tokens)
        logits = 2.0 * jnp.dot(normed, unit_keys, preferred_element_type=jnp.float32)
        powers = jnp.exp(logits)
        dispatch = (powers / lax.optimization_barrier(jnp.sum(powers, axis=0, keepdims=True))).astype(jnp.bfloat16)
        combine = (powers / lax.optimization_barrier(jnp.sum(powers, axis=1, keepdims=True))).astype(jnp.bfloat16)
        slot_in = lax.dot_general(dispatch, tokens, (((0,), (0,)), ((), ())), preferred_element_type=jnp.float32)
        return (slot_in.astype(jnp.bfloat16), combine)
    slot_in, combine = lax.map(mix_image, images_in)
    grouped = slot_in.reshape(IMAGES, EXPERTS, SLOTS, D)
    quarter = FF // N_HID

    def run_expert(expert_id):
        slot_rows = lax.dynamic_index_in_dim(grouped, expert_id, 1, keepdims=False)
        slot_rows = slot_rows.reshape(IMAGES * SLOTS, D).astype(jnp.float32)
        w_first = lax.dynamic_index_in_dim(w_in, expert_id, 0, keepdims=False).astype(jnp.float32).reshape(D, N_HID, quarter)
        w_second = lax.dynamic_index_in_dim(w_out, expert_id, 0, keepdims=False).astype(jnp.float32).reshape(N_HID, quarter, D)
        hidden = jax.nn.gelu(jnp.einsum('rd,dqf->rqf', slot_rows, w_first), approximate=True).astype(jnp.bfloat16)
        partial_value = jnp.einsum('rqf,qfd->rqd', hidden.astype(jnp.float32), w_second).astype(jnp.bfloat16)
        return lax.optimization_barrier(jnp.sum(partial_value.astype(jnp.float32), axis=1)).astype(jnp.bfloat16)
    slot_out = lax.map(run_expert, jnp.arange(EXPERTS, dtype=jnp.int32))
    slot_out = slot_out.reshape(EXPERTS, IMAGES, SLOTS, D).transpose(1, 0, 2, 3).reshape(IMAGES, EXPERTS * SLOTS, D)

    def combine_image(paired):
        return jnp.dot(paired[0], paired[1], preferred_element_type=jnp.float32).astype(jnp.bfloat16)
    return lax.map(combine_image, (combine, slot_out))
```

```python
import jax
import jax.numpy as jnp
from jax import lax
from jax.sharding import PartitionSpec as P

SLOTS = 2


def normal_rows(values):
    floats = values.astype(jnp.float32)
    return (floats * lax.rsqrt(jnp.mean(floats * floats, axis=-1, keepdims=True) + 1e-06)).astype(
        jnp.bfloat16
    )


def unit_columns(values):
    floats = values.astype(jnp.float32)
    return (floats * lax.rsqrt(jnp.sum(floats * floats, axis=0, keepdims=True) + 1e-06)).astype(
        jnp.bfloat16
    )


def shift(value, by):
    ring = lax.axis_size("hid")
    return lax.ppermute(value, "hid", [(i, (i + by) % ring) for i in range(ring)])


def plus(first, second):
    return (first.astype(jnp.float32) + second.astype(jnp.float32)).astype(jnp.bfloat16)


def expert(rows, w_in, w_out):
    flat = rows.reshape(-1, rows.shape[-1])
    hidden = jax.nn.gelu(
        jnp.dot(flat, w_in, preferred_element_type=jnp.float32), approximate=True
    ).astype(jnp.bfloat16)
    out = jnp.dot(hidden, w_out, preferred_element_type=jnp.float32).astype(jnp.bfloat16)
    return out.reshape(rows.shape)


def body(images_in, slot_keys, w_in, w_out):
    unit_keys = unit_columns(slot_keys)
    normed = normal_rows(images_in)
    logits = 2.0 * jnp.einsum("itd,de->ite", normed, unit_keys, preferred_element_type=jnp.float32)
    powers = jnp.exp(logits)
    dispatch = (powers / jnp.sum(powers, axis=1, keepdims=True)).astype(jnp.bfloat16)
    combine = (powers / jnp.sum(powers, axis=2, keepdims=True)).astype(jnp.bfloat16)
    slot_in = jnp.einsum(
        "ite,itd->ied", dispatch, images_in, preferred_element_type=jnp.float32
    ).astype(jnp.bfloat16)
    owners = lax.axis_size("expert")
    local_experts = w_in.shape[0]
    d_width = w_in.shape[1]
    half = owners // 2
    grouped = slot_in.reshape(owners, local_experts, SLOTS, d_width)
    results = []
    for b in range(local_experts):
        own = lax.all_to_all(grouped[:, b], "expert", 0, 0, tiled=True)
        left, right = shift(own, 1), shift(own, -1)
        far = jnp.concatenate([shift(left[:half], 1), shift(right[half:], -1)])
        near_out = expert(jnp.concatenate([own, left, right]), w_in[b], w_out[b])
        far_out = expert(far, w_in[b], w_out[b])
        own_out, left_out, right_out = jnp.split(near_out, 3)
        low, high = shift(far_out[:half], 1), shift(far_out[half:], -1)
        to_right = jnp.concatenate([plus(right_out[:half], low), right_out[half:]])
        to_left = jnp.concatenate([left_out[:half], plus(left_out[half:], high)])
        from_left, from_right = shift(to_right, 1), shift(to_left, -1)
        summed = (
            own_out.astype(jnp.float32)
            + from_left.astype(jnp.float32)
            + from_right.astype(jnp.float32)
        ).astype(jnp.bfloat16)
        results.append(lax.all_to_all(summed, "expert", 0, 0, tiled=True))
    results = jnp.stack(results, axis=1).reshape(1, -1, d_width)
    return jnp.einsum("ite,ied->itd", combine, results, preferred_element_type=jnp.float32).astype(
        jnp.bfloat16
    )


def solution(mesh):
    return jax.shard_map(
        body,
        mesh=mesh,
        in_specs=(
            P(("dp", "expert", "hid"), None, None),
            P(),
            P("expert", None, "hid"),
            P("expert", "hid", None),
        ),
        out_specs=P(("dp", "expert", "hid"), None, None),
        check_vma=False,
    )
```

```python
import jax
import jax.numpy as jnp
from jax import lax
from jax.sharding import PartitionSpec as P

SLOTS = 2


def normal_rows(values):
    floats = values.astype(jnp.float32)
    return (floats * lax.rsqrt(jnp.mean(floats * floats, axis=-1, keepdims=True) + 1e-06)).astype(
        jnp.bfloat16
    )


def unit_columns(values):
    floats = values.astype(jnp.float32)
    return (floats * lax.rsqrt(jnp.sum(floats * floats, axis=0, keepdims=True) + 1e-06)).astype(
        jnp.bfloat16
    )


def onward(value):
    groups, ring = lax.axis_size("dp"), lax.axis_size("hid")
    pairs = []
    for group in range(groups):
        step = 1 if group % 2 == 0 else ring - 1
        pairs += [(group * ring + i, group * ring + (i + step) % ring) for i in range(ring)]
    return lax.ppermute(value, ("dp", "hid"), pairs)


def expert(rows, w_in, w_out, arrived=None):
    hidden = jax.nn.gelu(
        jnp.dot(rows, w_in, preferred_element_type=jnp.float32), approximate=True
    ).astype(jnp.bfloat16)
    out = jnp.dot(hidden, w_out, preferred_element_type=jnp.float32)
    if arrived is not None:
        out = out + arrived.astype(jnp.float32)
    return out.astype(jnp.bfloat16)


def body(images_in, slot_keys, w_in, w_out):
    unit_keys = unit_columns(slot_keys)
    normed = normal_rows(images_in)
    logits = 2.0 * jnp.einsum("itd,de->ite", normed, unit_keys, preferred_element_type=jnp.float32)
    powers = jnp.exp(logits)
    dispatch = (powers / jnp.sum(powers, axis=1, keepdims=True)).astype(jnp.bfloat16)
    combine = (powers / jnp.sum(powers, axis=2, keepdims=True)).astype(jnp.bfloat16)
    slot_in = jnp.einsum(
        "ite,itd->ied", dispatch, images_in, preferred_element_type=jnp.float32
    ).astype(jnp.bfloat16)
    owners = lax.axis_size("expert")
    local_experts = w_in.shape[0]
    d_width = w_in.shape[1]
    grouped = slot_in.reshape(owners, local_experts, SLOTS, d_width)
    results = []
    for b in range(local_experts):
        own = lax.all_to_all(grouped[:, b], "expert", 0, 0, tiled=True).reshape(-1, d_width)
        block, total = own, None
        for _ in range(lax.axis_size("hid") - 1):
            block = onward(block)
            total = onward(expert(block, w_in[b], w_out[b], total))
        total = expert(own, w_in[b], w_out[b], total)
        total = total.reshape(owners, SLOTS, d_width)
        results.append(lax.all_to_all(total, "expert", 0, 0, tiled=True))
    results = jnp.stack(results, axis=1).reshape(1, -1, d_width)
    return jnp.einsum("ite,ied->itd", combine, results, preferred_element_type=jnp.float32).astype(
        jnp.bfloat16
    )


def solution(mesh):
    return jax.shard_map(
        body,
        mesh=mesh,
        in_specs=(
            P(("dp", "expert", "hid"), None, None),
            P(),
            P("expert", None, "hid"),
            P("expert", "hid", None),
        ),
        out_specs=P(("dp", "expert", "hid"), None, None),
        check_vma=False,
    )
```

```python
import jax
import jax.numpy as jnp
from jax import lax
from jax.sharding import PartitionSpec as P

SLOTS = 2


def normal_rows(values):
    floats = values.astype(jnp.float32)
    return (floats * lax.rsqrt(jnp.mean(floats * floats, axis=-1, keepdims=True) + 1e-06)).astype(
        jnp.bfloat16
    )


def unit_columns(values):
    floats = values.astype(jnp.float32)
    return (floats * lax.rsqrt(jnp.sum(floats * floats, axis=0, keepdims=True) + 1e-06)).astype(
        jnp.bfloat16
    )


def swap(value, masks):
    groups, ring = lax.axis_size("dp"), lax.axis_size("hid")
    pairs = [
        (group * ring + i, group * ring + (i ^ masks[group % 2]))
        for group in range(groups)
        for i in range(ring)
    ]
    return lax.ppermute(value, ("dp", "hid"), pairs)


def near(value):
    return swap(value, (1, 3))


def far(value):
    return swap(value, (3, 1))


def expert(rows, w_in, w_out):
    hidden = jax.nn.gelu(
        jnp.dot(rows, w_in, preferred_element_type=jnp.float32), approximate=True
    ).astype(jnp.bfloat16)
    return jnp.dot(hidden, w_out, preferred_element_type=jnp.float32)


def exchange(own, w_in, w_out):
    count = own.shape[0]
    beside = near(own)
    pair = jnp.concatenate([own, beside])
    others = far(pair)
    others, here = lax.optimization_barrier((others, expert(pair, w_in, w_out)))
    there = expert(others, w_in, w_out).astype(jnp.bfloat16)
    back = far(there)
    total = here + back.astype(jnp.float32)
    total, rest = total[:count], total[count:].astype(jnp.bfloat16)
    rest = near(rest)
    return (total + rest.astype(jnp.float32)).astype(jnp.bfloat16)


def layer(images_in, slot_keys, w_in, w_out):
    unit_keys = unit_columns(slot_keys)
    normed = normal_rows(images_in)
    logits = 2.0 * jnp.einsum("itd,de->ite", normed, unit_keys, preferred_element_type=jnp.float32)
    powers = jnp.exp(logits)
    dispatch = (powers / jnp.sum(powers, axis=1, keepdims=True)).astype(jnp.bfloat16)
    combine = (powers / jnp.sum(powers, axis=2, keepdims=True)).astype(jnp.bfloat16)
    slot_in = jnp.einsum(
        "ite,itd->ied", dispatch, images_in, preferred_element_type=jnp.float32
    ).astype(jnp.bfloat16)
    owners = lax.axis_size("expert")
    local_experts = w_in.shape[0]
    d_width = w_in.shape[1]
    grouped = slot_in.reshape(owners, local_experts, SLOTS, d_width)
    arrived = lax.all_to_all(grouped, "expert", 0, 0, tiled=True)
    results = []
    for b in range(local_experts):
        own = arrived[:, b].reshape(-1, d_width)
        results.append(exchange(own, w_in[b], w_out[b]).reshape(owners, SLOTS, d_width))
    results = lax.all_to_all(jnp.stack(results, axis=1), "expert", 0, 0, tiled=True)
    results = results.reshape(1, -1, d_width)
    return jnp.einsum("ite,ied->itd", combine, results, preferred_element_type=jnp.float32).astype(
        jnp.bfloat16
    )


def solution(mesh):
    return jax.shard_map(
        layer,
        mesh=mesh,
        in_specs=(
            P(("dp", "expert", "hid"), None, None),
            P(),
            P("expert", None, "hid"),
            P("expert", "hid", None),
        ),
        out_specs=P(("dp", "expert", "hid"), None, None),
        check_vma=False,
    )
```

```python
import jax
import jax.numpy as jnp
from jax import lax
from jax.sharding import PartitionSpec as P

SLOTS = 2
RUN = 8


def normal_rows(values):
    floats = values.astype(jnp.float32)
    return (floats * lax.rsqrt(jnp.mean(floats * floats, axis=-1, keepdims=True) + 1e-06)).astype(
        jnp.bfloat16
    )


def unit_columns(values):
    floats = values.astype(jnp.float32)
    return (floats * lax.rsqrt(jnp.sum(floats * floats, axis=0, keepdims=True) + 1e-06)).astype(
        jnp.bfloat16
    )


def swap(value, masks):
    groups, ring = lax.axis_size("dp"), lax.axis_size("hid")
    pairs = [
        (group * ring + i, group * ring + (i ^ masks[group % 2]))
        for group in range(groups)
        for i in range(ring)
    ]
    return lax.ppermute(value, ("dp", "hid"), pairs)


def to_owners(value):
    groups, owners, ring = (lax.axis_size(name) for name in ("dp", "expert", "hid"))
    teams = [
        [
            (group * owners + owner) * ring
            + (member + (group % 2 == 1 and owner % RUN < RUN // 2)) % ring
            for owner in range(owners)
        ]
        for group in range(groups)
        for member in range(ring)
    ]
    return lax.all_to_all(
        value, ("dp", "expert", "hid"), 0, 0, axis_index_groups=teams, tiled=True
    )


def near(value):
    return swap(value, (1, 3))


def far(value):
    return swap(value, (3, 1))


def expert(rows, w_in, w_out):
    hidden = jax.nn.gelu(
        jnp.dot(rows, w_in, preferred_element_type=jnp.float32), approximate=True
    ).astype(jnp.bfloat16)
    return jnp.dot(hidden, w_out, preferred_element_type=jnp.float32)


def exchange(own, w_in, w_out):
    count = own.shape[0]
    beside = near(own)
    pair = jnp.concatenate([own, beside])
    others = far(pair)
    others, here = lax.optimization_barrier((others, expert(pair, w_in, w_out)))
    there = expert(others, w_in, w_out).astype(jnp.bfloat16)
    back = far(there)
    total = here + back.astype(jnp.float32)
    total, rest = total[:count], total[count:].astype(jnp.bfloat16)
    rest = near(rest)
    return (total + rest.astype(jnp.float32)).astype(jnp.bfloat16)


def layer(images_in, slot_keys, w_in, w_out):
    unit_keys = unit_columns(slot_keys)
    normed = normal_rows(images_in)
    logits = 2.0 * jnp.einsum("itd,de->ite", normed, unit_keys, preferred_element_type=jnp.float32)
    powers = jnp.exp(logits)
    dispatch = (powers / jnp.sum(powers, axis=1, keepdims=True)).astype(jnp.bfloat16)
    combine = (powers / jnp.sum(powers, axis=2, keepdims=True)).astype(jnp.bfloat16)
    slot_in = jnp.einsum(
        "ite,itd->ied", dispatch, images_in, preferred_element_type=jnp.float32
    ).astype(jnp.bfloat16)
    owners = lax.axis_size("expert")
    local_experts = w_in.shape[0]
    d_width = w_in.shape[1]
    grouped = slot_in.reshape(owners, local_experts, SLOTS, d_width)
    arrived = to_owners(grouped)
    results = []
    for b in range(local_experts):
        own = arrived[:, b].reshape(-1, d_width)
        results.append(exchange(own, w_in[b], w_out[b]).reshape(owners, SLOTS, d_width))
    results = to_owners(jnp.stack(results, axis=1))
    results = results.reshape(1, -1, d_width)
    return jnp.einsum("ite,ied->itd", combine, results, preferred_element_type=jnp.float32).astype(
        jnp.bfloat16
    )


def solution(mesh):
    return jax.shard_map(
        layer,
        mesh=mesh,
        in_specs=(
            P(("dp", "expert", "hid"), None, None),
            P(),
            P("expert", None, "hid"),
            P("expert", "hid", None),
        ),
        out_specs=P(("dp", "expert", "hid"), None, None),
        check_vma=False,
    )
```

```python
import jax
import jax.numpy as jnp
from jax import lax
from jax.experimental import pallas as pl
from jax.experimental.pallas import tpu as pltpu
from jax.sharding import PartitionSpec as P

SLOTS = 2
RUN = 8


def route(images_ref, keys_ref, slots_ref, combine_ref):
    keys = keys_ref[...].astype(jnp.float32)
    unit_keys = (keys * lax.rsqrt(jnp.sum(keys * keys, axis=0, keepdims=True) + 1e-06)).astype(
        jnp.bfloat16
    )
    tokens = images_ref[...]
    floats = tokens.astype(jnp.float32)
    normed = (floats * lax.rsqrt(jnp.mean(floats * floats, axis=1, keepdims=True) + 1e-06)).astype(
        jnp.bfloat16
    )
    powers = jnp.exp(2.0 * jnp.dot(normed, unit_keys, preferred_element_type=jnp.float32))
    dispatch = (powers / jnp.sum(powers, axis=0, keepdims=True)).astype(jnp.bfloat16)
    combine_ref[...] = (powers / jnp.sum(powers, axis=1, keepdims=True)).astype(jnp.bfloat16)
    slots_ref[...] = lax.dot_general(
        dispatch, tokens, (((0,), (0,)), ((), ())), preferred_element_type=jnp.float32
    ).astype(jnp.bfloat16)


def router(tokens, slot_keys):
    (rows, width), columns = tokens.shape, slot_keys.shape[1]
    return pl.pallas_call(
        route,
        out_shape=(
            jax.ShapeDtypeStruct((columns, width), jnp.bfloat16),
            jax.ShapeDtypeStruct((rows, columns), jnp.bfloat16),
        ),
        compiler_params=pltpu.CompilerParams(vmem_limit_bytes=60 << 20),
    )(tokens, slot_keys)


def onward(value):
    groups, ring = lax.axis_size("dp"), lax.axis_size("hid")
    pairs = []
    for group in range(groups):
        step = 1 if group % 2 == 0 else ring - 1
        pairs += [(group * ring + i, group * ring + (i + step) % ring) for i in range(ring)]
    return lax.ppermute(value, ("dp", "hid"), pairs)


def to_owners(value):
    groups, owners, ring = (lax.axis_size(name) for name in ("dp", "expert", "hid"))
    teams = [
        [
            (group * owners + owner) * ring
            + (member + (group % 2 == 1 and owner % RUN < RUN // 2)) % ring
            for owner in range(owners)
        ]
        for group in range(groups)
        for member in range(ring)
    ]
    return lax.all_to_all(
        value, ("dp", "expert", "hid"), 0, 0, axis_index_groups=teams, tiled=True
    )


def expert(rows, w_in, w_out):
    hidden = jax.nn.gelu(
        jnp.dot(rows, w_in, preferred_element_type=jnp.float32), approximate=True
    ).astype(jnp.bfloat16)
    return jnp.dot(hidden, w_out, preferred_element_type=jnp.float32)


def rings(owns, w_in, w_out):
    count, stops, chunks = owns[0].shape[0], lax.axis_size("hid"), range(len(owns))
    blocks = [onward(owns[c]) for c in chunks]
    totals = [expert(blocks[c], w_in[c], w_out[c]).astype(jnp.bfloat16) for c in chunks]
    for step in range(2, stops):
        for c in chunks:
            both = onward(jnp.concatenate([blocks[c], totals[c]]))
            if step == stops - 1 and c > 0:
                both, _ = lax.optimization_barrier((both, totals[c - 1]))
            blocks[c], total = both[:count], both[count:].astype(jnp.float32)
            if step < stops - 1:
                totals[c] = (expert(blocks[c], w_in[c], w_out[c]) + total).astype(jnp.bfloat16)
            else:
                last = expert(jnp.concatenate([blocks[c], owns[c]]), w_in[c], w_out[c])
                totals[c] = (last[:count] + total).astype(jnp.bfloat16)
                blocks[c] = last[count:]
    totals = [onward(totals[c]).astype(jnp.float32) for c in chunks]
    return [(blocks[c] + totals[c]).astype(jnp.bfloat16) for c in chunks]


def layer(images_in, slot_keys, w_in, w_out):
    slot_in, combine = router(images_in[0], slot_keys)
    owners = lax.axis_size("expert")
    local_experts = w_in.shape[0]
    d_width = w_in.shape[1]
    grouped = slot_in.reshape(owners, local_experts, SLOTS, d_width)
    arrived = to_owners(grouped)
    owns = [arrived[:, b].reshape(-1, d_width) for b in range(local_experts)]
    results = [total.reshape(owners, SLOTS, d_width) for total in rings(owns, w_in, w_out)]
    results = to_owners(jnp.stack(results, axis=1))
    results = results.reshape(-1, d_width)
    mixed = jnp.dot(combine, results, preferred_element_type=jnp.float32)
    return mixed.astype(jnp.bfloat16)[None]


def solution(mesh):
    return jax.shard_map(
        layer,
        mesh=mesh,
        in_specs=(
            P(("dp", "expert", "hid"), None, None),
            P(),
            P("expert", None, "hid"),
            P("expert", "hid", None),
        ),
        out_specs=P(("dp", "expert", "hid"), None, None),
        check_vma=False,
    )
```

```python
import functools

import jax
import jax.numpy as jnp
from jax import lax
from jax.experimental import pallas as pl
from jax.experimental.pallas import tpu as pltpu
from jax.sharding import PartitionSpec as P

SLOTS = 2
RUN = 8
VMEM = 16 << 20


def route(images_ref, keys_ref, slots_ref, combine_ref):
    keys = keys_ref[...].astype(jnp.float32)
    unit_keys = (keys * lax.rsqrt(jnp.sum(keys * keys, axis=0, keepdims=True) + 1e-06)).astype(
        jnp.bfloat16
    )
    tokens = images_ref[...]
    floats = tokens.astype(jnp.float32)
    normed = (floats * lax.rsqrt(jnp.mean(floats * floats, axis=1, keepdims=True) + 1e-06)).astype(
        jnp.bfloat16
    )
    powers = jnp.exp(2.0 * jnp.dot(normed, unit_keys, preferred_element_type=jnp.float32))
    dispatch = (powers / jnp.sum(powers, axis=0, keepdims=True)).astype(jnp.bfloat16)
    combine_ref[...] = (powers / jnp.sum(powers, axis=1, keepdims=True)).astype(jnp.bfloat16)
    slots_ref[...] = lax.dot_general(
        dispatch, tokens, (((0,), (0,)), ((), ())), preferred_element_type=jnp.float32
    ).astype(jnp.bfloat16)


def router(tokens, slot_keys):
    (rows, width), columns = tokens.shape, slot_keys.shape[1]
    return pl.pallas_call(
        route,
        out_shape=(
            jax.ShapeDtypeStruct((columns, width), jnp.bfloat16),
            jax.ShapeDtypeStruct((rows, columns), jnp.bfloat16),
        ),
        compiler_params=pltpu.CompilerParams(vmem_limit_bytes=60 << 20),
    )(tokens, slot_keys)


def onward(value):
    groups, ring = lax.axis_size("dp"), lax.axis_size("hid")
    pairs = []
    for group in range(groups):
        step = 1 if group % 2 == 0 else ring - 1
        pairs += [(group * ring + i, group * ring + (i + step) % ring) for i in range(ring)]
    return lax.ppermute(value, ("dp", "hid"), pairs)


def to_owners(value):
    groups, owners, ring = (lax.axis_size(name) for name in ("dp", "expert", "hid"))
    teams = [
        [
            (group * owners + owner) * ring
            + (member + (group % 2 == 1 and owner % RUN < RUN // 2)) % ring
            for owner in range(owners)
        ]
        for group in range(groups)
        for member in range(ring)
    ]
    return lax.all_to_all(
        value, ("dp", "expert", "hid"), 0, 0, axis_index_groups=teams, tiled=True
    )


def apply(count, add, *refs):
    rows_ref, w_in_ref, w_out_ref = refs[:3]
    arrived_ref = refs[3] if add else None
    total_ref, acc_ref = refs[3 + add], refs[-1]
    step, last = pl.program_id(0), pl.num_programs(0) - 1
    hidden = jax.nn.gelu(
        jnp.dot(rows_ref[...], w_in_ref[...], preferred_element_type=jnp.float32),
        approximate=True,
    ).astype(jnp.bfloat16)
    part = jnp.dot(hidden, w_out_ref[...], preferred_element_type=jnp.float32)

    @pl.when(step == 0)
    def _():
        acc_ref[...] = part

    @pl.when(step > 0)
    def _():
        acc_ref[...] += part

    @pl.when(step == last)
    def _():
        total = acc_ref[:count, :]
        if add:
            total = total + arrived_ref[...].astype(jnp.float32)
        total_ref[...] = total.astype(jnp.bfloat16)
        if rows_ref.shape[0] > count:
            refs[4 + add][...] = acc_ref[count:, :]


def expert(which, rows, w_in, w_out, arrived=None, keep=0):
    size, width = rows.shape
    units, count, tile = w_in.shape[2], size - keep, w_in.shape[2] // 4
    add = arrived is not None
    out_shape = [jax.ShapeDtypeStruct((count, width), jnp.bfloat16)]
    if keep:
        out_shape.append(jax.ShapeDtypeStruct((keep, width), jnp.float32))
    whole = lambda height: pl.BlockSpec((height, width), lambda j: (0, 0))
    outs = pl.pallas_call(
        functools.partial(apply, count, add),
        grid=(units // tile,),
        out_shape=out_shape,
        in_specs=[
            whole(size),
            pl.BlockSpec((None, width, tile), lambda j: (which, 0, j)),
            pl.BlockSpec((None, tile, width), lambda j: (which, j, 0)),
        ]
        + [whole(count)] * add,
        out_specs=[whole(shape.shape[0]) for shape in out_shape],
        scratch_shapes=[pltpu.VMEM((size, width), jnp.float32)],
        cost_estimate=pl.CostEstimate(
            flops=4 * size * width * units,
            bytes_accessed=4 * width * units,
            transcendentals=size * units,
        ),
        compiler_params=pltpu.CompilerParams(vmem_limit_bytes=VMEM),
    )(rows, w_in, w_out, *([arrived] if add else []))
    return outs if keep else outs[0]


def rings(owns, w_in, w_out):
    stops, chunks = lax.axis_size("hid"), range(len(owns))
    blocks = [onward(owns[c]) for c in chunks]
    totals, kept, mark = [None for c in chunks], [None for c in chunks], None
    for step in range(1, stops):
        for c in chunks:
            block = blocks[c]
            if mark is not None:
                block, _ = lax.optimization_barrier((block, mark))
            if step < stops - 1:
                blocks[c] = onward(block)
                mark = expert(c, block, w_in, w_out, totals[c])
            else:
                rows = jnp.concatenate([block, owns[c]])
                mark, kept[c] = expert(c, rows, w_in, w_out, totals[c], owns[c].shape[0])
            totals[c] = onward(mark)
    return [(kept[c] + totals[c].astype(jnp.float32)).astype(jnp.bfloat16) for c in chunks]


def layer(images_in, slot_keys, w_in, w_out):
    slot_in, combine = router(images_in[0], slot_keys)
    owners = lax.axis_size("expert")
    local_experts = w_in.shape[0]
    d_width = w_in.shape[1]
    grouped = slot_in.reshape(owners, local_experts, SLOTS, d_width)
    arrived = to_owners(grouped)
    owns = [arrived[:, b].reshape(-1, d_width) for b in range(local_experts)]
    results = [total.reshape(owners, SLOTS, d_width) for total in rings(owns, w_in, w_out)]
    results = to_owners(jnp.stack(results, axis=1))
    results = results.reshape(-1, d_width)
    mixed = jnp.dot(combine, results, preferred_element_type=jnp.float32)
    return mixed.astype(jnp.bfloat16)[None]


def solution(mesh):
    return jax.shard_map(
        layer,
        mesh=mesh,
        in_specs=(
            P(("dp", "expert", "hid"), None, None),
            P(),
            P("expert", None, "hid"),
            P("expert", "hid", None),
        ),
        out_specs=P(("dp", "expert", "hid"), None, None),
        check_vma=False,
    )
```

```python
import functools

import jax
import jax.numpy as jnp
from jax import lax
from jax.experimental import pallas as pl
from jax.experimental.pallas import tpu as pltpu
from jax.sharding import PartitionSpec as P

SLOTS = 2
RUN = 8
VMEM = 16 << 20


def in_hbm(value):
    return pltpu.with_memory_space_constraint(value, pltpu.HBM)


def route(images_ref, keys_ref, slots_ref, combine_ref):
    keys = keys_ref[...].astype(jnp.float32)
    unit_keys = (keys * lax.rsqrt(jnp.sum(keys * keys, axis=0, keepdims=True) + 1e-06)).astype(
        jnp.bfloat16
    )
    tokens = images_ref[...]
    floats = tokens.astype(jnp.float32)
    normed = (floats * lax.rsqrt(jnp.mean(floats * floats, axis=1, keepdims=True) + 1e-06)).astype(
        jnp.bfloat16
    )
    powers = jnp.exp(2.0 * jnp.dot(normed, unit_keys, preferred_element_type=jnp.float32))
    dispatch = (powers / jnp.sum(powers, axis=0, keepdims=True)).astype(jnp.bfloat16)
    combine_ref[...] = (powers / jnp.sum(powers, axis=1, keepdims=True)).astype(jnp.bfloat16)
    slots_ref[...] = lax.dot_general(
        dispatch, tokens, (((0,), (0,)), ((), ())), preferred_element_type=jnp.float32
    ).astype(jnp.bfloat16)


def router(tokens, slot_keys):
    (rows, width), columns = tokens.shape, slot_keys.shape[1]
    return pl.pallas_call(
        route,
        out_shape=(
            jax.ShapeDtypeStruct((columns, width), jnp.bfloat16),
            jax.ShapeDtypeStruct((rows, columns), jnp.bfloat16),
        ),
        compiler_params=pltpu.CompilerParams(vmem_limit_bytes=VMEM),
    )(in_hbm(tokens), in_hbm(slot_keys))


def onward(value):
    groups, ring = lax.axis_size("dp"), lax.axis_size("hid")
    pairs = []
    for group in range(groups):
        step = 1 if group % 2 == 0 else ring - 1
        pairs += [(group * ring + i, group * ring + (i + step) % ring) for i in range(ring)]
    return lax.ppermute(value, ("dp", "hid"), pairs)


def to_owners(value):
    groups, owners, ring = (lax.axis_size(name) for name in ("dp", "expert", "hid"))
    teams = [
        [
            (group * owners + owner) * ring
            + (member + (group % 2 == 1 and owner % RUN < RUN // 2)) % ring
            for owner in range(owners)
        ]
        for group in range(groups)
        for member in range(ring)
    ]
    return lax.all_to_all(
        value, ("dp", "expert", "hid"), 0, 0, axis_index_groups=teams, tiled=True
    )


def apply(count, add, *refs):
    rows_ref, w_in_ref, w_out_ref = refs[:3]
    arrived_ref = refs[3] if add else None
    total_ref, acc_ref = refs[3 + add], refs[-1]
    step, last = pl.program_id(0), pl.num_programs(0) - 1
    hidden = jax.nn.gelu(
        jnp.dot(rows_ref[...], w_in_ref[...], preferred_element_type=jnp.float32),
        approximate=True,
    ).astype(jnp.bfloat16)
    part = jnp.dot(hidden, w_out_ref[...], preferred_element_type=jnp.float32)

    @pl.when(step == 0)
    def _():
        acc_ref[...] = part

    @pl.when(step > 0)
    def _():
        acc_ref[...] += part

    @pl.when(step == last)
    def _():
        total = acc_ref[:count, :]
        if add:
            total = total + arrived_ref[...].astype(jnp.float32)
        total_ref[...] = total.astype(jnp.bfloat16)
        if rows_ref.shape[0] > count:
            refs[4 + add][...] = acc_ref[count:, :]


def expert(which, rows, w_in, w_out, arrived=None, keep=0):
    size, width = rows.shape
    units, count, tile = w_in.shape[2], size - keep, w_in.shape[2] // 4
    add = arrived is not None
    out_shape = [jax.ShapeDtypeStruct((count, width), jnp.bfloat16)]
    if keep:
        out_shape.append(jax.ShapeDtypeStruct((keep, width), jnp.float32))
    whole = lambda height: pl.BlockSpec((height, width), lambda j: (0, 0))
    outs = pl.pallas_call(
        functools.partial(apply, count, add),
        grid=(units // tile,),
        out_shape=out_shape,
        in_specs=[
            whole(size),
            pl.BlockSpec((None, width, tile), lambda j: (which, 0, j)),
            pl.BlockSpec((None, tile, width), lambda j: (which, j, 0)),
        ]
        + [whole(count)] * add,
        out_specs=[whole(shape.shape[0]) for shape in out_shape],
        scratch_shapes=[pltpu.VMEM((size, width), jnp.float32)],
        cost_estimate=pl.CostEstimate(
            flops=4 * size * width * units,
            bytes_accessed=4 * width * units,
            transcendentals=size * units,
        ),
        compiler_params=pltpu.CompilerParams(vmem_limit_bytes=VMEM),
    )(rows, in_hbm(w_in), in_hbm(w_out), *([arrived] if add else []))
    return outs if keep else outs[0]


def rings(owns, w_in, w_out):
    stops, chunks = lax.axis_size("hid"), range(len(owns))
    blocks = [onward(owns[c]) for c in chunks]
    totals, kept, mark = [None for c in chunks], [None for c in chunks], None
    for step in range(1, stops):
        for c in chunks:
            block = blocks[c]
            if mark is not None:
                block, _ = lax.optimization_barrier((block, mark))
            if step < stops - 1:
                blocks[c] = onward(block)
                mark = expert(c, block, w_in, w_out, totals[c])
            else:
                rows = jnp.concatenate([block, owns[c]])
                mark, kept[c] = expert(c, rows, w_in, w_out, totals[c], owns[c].shape[0])
            totals[c] = onward(mark)
    return [(kept[c] + totals[c].astype(jnp.float32)).astype(jnp.bfloat16) for c in chunks]


def layer(images_in, slot_keys, w_in, w_out):
    slot_in, combine = router(images_in[0], slot_keys)
    owners = lax.axis_size("expert")
    local_experts = w_in.shape[0]
    d_width = w_in.shape[1]
    grouped = slot_in.reshape(owners, local_experts, SLOTS, d_width)
    arrived = to_owners(grouped)
    owns = [arrived[:, b].reshape(-1, d_width) for b in range(local_experts)]
    results = [total.reshape(owners, SLOTS, d_width) for total in rings(owns, w_in, w_out)]
    results = to_owners(jnp.stack(results, axis=1))
    results = results.reshape(-1, d_width)
    mixed = jnp.dot(combine, results, preferred_element_type=jnp.float32)
    return mixed.astype(jnp.bfloat16)[None]


def solution(mesh):
    return jax.shard_map(
        layer,
        mesh=mesh,
        in_specs=(
            P(("dp", "expert", "hid"), None, None),
            P(),
            P("expert", None, "hid"),
            P("expert", "hid", None),
        ),
        out_specs=P(("dp", "expert", "hid"), None, None),
        check_vma=False,
    )
```

```python
import functools

import jax
import jax.numpy as jnp
from jax import lax
from jax.experimental import pallas as pl
from jax.experimental.pallas import tpu as pltpu
from jax.sharding import PartitionSpec as P

SLOTS = 2
RUN = 8
VMEM = 16 << 20


def in_hbm(value):
    return pltpu.with_memory_space_constraint(value, pltpu.HBM)


def route(images_ref, keys_ref, slots_ref, combine_ref):
    keys = keys_ref[...].astype(jnp.float32)
    unit_keys = (keys * lax.rsqrt(jnp.sum(keys * keys, axis=0, keepdims=True) + 1e-06)).astype(
        jnp.bfloat16
    )
    tokens = images_ref[...]
    floats = tokens.astype(jnp.float32)
    normed = (floats * lax.rsqrt(jnp.mean(floats * floats, axis=1, keepdims=True) + 1e-06)).astype(
        jnp.bfloat16
    )
    powers = jnp.exp(2.0 * jnp.dot(normed, unit_keys, preferred_element_type=jnp.float32))
    dispatch = (powers / jnp.sum(powers, axis=0, keepdims=True)).astype(jnp.bfloat16)
    combine_ref[...] = (powers / jnp.sum(powers, axis=1, keepdims=True)).astype(jnp.bfloat16)
    slots_ref[...] = lax.dot_general(
        dispatch, tokens, (((0,), (0,)), ((), ())), preferred_element_type=jnp.float32
    ).astype(jnp.bfloat16)


def router(tokens, slot_keys):
    (rows, width), columns = tokens.shape, slot_keys.shape[1]
    return pl.pallas_call(
        route,
        out_shape=(
            jax.ShapeDtypeStruct((columns, width), jnp.bfloat16),
            jax.ShapeDtypeStruct((rows, columns), jnp.bfloat16),
        ),
        compiler_params=pltpu.CompilerParams(vmem_limit_bytes=VMEM),
    )(in_hbm(tokens), in_hbm(slot_keys))


def onward(value):
    groups, ring = lax.axis_size("dp"), lax.axis_size("hid")
    pairs = []
    for group in range(groups):
        step = 1 if group % 2 == 0 else ring - 1
        pairs += [(group * ring + i, group * ring + (i + step) % ring) for i in range(ring)]
    return lax.ppermute(value, ("dp", "hid"), pairs)


def to_owners(value):
    groups, owners, ring = (lax.axis_size(name) for name in ("dp", "expert", "hid"))
    teams = [
        [
            (group * owners + owner) * ring
            + (member + (group % 2 == 1 and owner % RUN < RUN // 2)) % ring
            for owner in range(owners)
        ]
        for group in range(groups)
        for member in range(ring)
    ]
    return lax.all_to_all(
        value, ("dp", "expert", "hid"), 0, 0, axis_index_groups=teams, tiled=True
    )


def apply(count, add, *refs):
    rows_ref, w_in_ref, w_out_ref = refs[:3]
    arrived_ref = refs[3] if add else None
    total_ref, acc_ref = refs[3 + add], refs[-1]
    step, last = pl.program_id(0), pl.num_programs(0) - 1
    hidden = jax.nn.gelu(
        jnp.dot(rows_ref[...], w_in_ref[...], preferred_element_type=jnp.float32),
        approximate=True,
    ).astype(jnp.bfloat16)
    part = jnp.dot(hidden, w_out_ref[...], preferred_element_type=jnp.float32)

    @pl.when(step == 0)
    def _():
        acc_ref[...] = part

    @pl.when(step > 0)
    def _():
        acc_ref[...] += part

    @pl.when(step == last)
    def _():
        total = acc_ref[:count, :]
        if add:
            total = total + arrived_ref[...].astype(jnp.float32)
        total_ref[...] = total.astype(jnp.bfloat16)
        if rows_ref.shape[0] > count:
            refs[4 + add][...] = acc_ref[count:, :]


def expert(which, rows, w_in, w_out, arrived=None, keep=0):
    size, width = rows.shape
    units, count, tile = w_in.shape[2], size - keep, w_in.shape[2] // 4
    add = arrived is not None
    out_shape = [jax.ShapeDtypeStruct((count, width), jnp.bfloat16)]
    if keep:
        out_shape.append(jax.ShapeDtypeStruct((keep, width), jnp.float32))
    whole = lambda height: pl.BlockSpec((height, width), lambda j: (0, 0))
    outs = pl.pallas_call(
        functools.partial(apply, count, add),
        grid=(units // tile,),
        out_shape=out_shape,
        in_specs=[
            whole(size),
            pl.BlockSpec((None, width, tile), lambda j: (which, 0, j)),
            pl.BlockSpec((None, tile, width), lambda j: (which, j, 0)),
        ]
        + [whole(count)] * add,
        out_specs=[whole(shape.shape[0]) for shape in out_shape],
        scratch_shapes=[pltpu.VMEM((size, width), jnp.float32)],
        cost_estimate=pl.CostEstimate(
            flops=4 * size * width * units,
            bytes_accessed=4 * width * units,
            transcendentals=size * units,
        ),
        compiler_params=pltpu.CompilerParams(vmem_limit_bytes=VMEM),
    )(rows, w_in, w_out, *([arrived] if add else []))
    return outs if keep else outs[0]


def rings(owns, w_in, w_out):
    stops, chunks = lax.axis_size("hid"), range(len(owns))
    blocks = [onward(owns[c]) for c in chunks]
    totals, kept, mark = [None for c in chunks], [None for c in chunks], None
    for step in range(1, stops):
        for c in chunks:
            block = blocks[c]
            if mark is not None:
                block, _ = lax.optimization_barrier((block, mark))
            if step < stops - 1:
                blocks[c] = onward(block)
                first = step == 1 and c == 0
                weights = [in_hbm(w) if first else w for w in (w_in, w_out)]
                mark = expert(c, block, *weights, totals[c])
            else:
                rows = jnp.concatenate([block, owns[c]])
                mark, kept[c] = expert(c, rows, w_in, w_out, totals[c], owns[c].shape[0])
            totals[c] = onward(mark)
    return [(kept[c] + totals[c].astype(jnp.float32)).astype(jnp.bfloat16) for c in chunks]


def layer(images_in, slot_keys, w_in, w_out):
    slot_in, combine = router(images_in[0], slot_keys)
    owners = lax.axis_size("expert")
    local_experts = w_in.shape[0]
    d_width = w_in.shape[1]
    grouped = slot_in.reshape(owners, local_experts, SLOTS, d_width)
    arrived = to_owners(grouped)
    owns = [arrived[:, b].reshape(-1, d_width) for b in range(local_experts)]
    results = [total.reshape(owners, SLOTS, d_width) for total in rings(owns, w_in, w_out)]
    results = to_owners(jnp.stack(results, axis=1))
    results = results.reshape(-1, d_width)
    mixed = jnp.dot(combine, results, preferred_element_type=jnp.float32)
    return mixed.astype(jnp.bfloat16)[None]


def solution(mesh):
    return jax.shard_map(
        layer,
        mesh=mesh,
        in_specs=(
            P(("dp", "expert", "hid"), None, None),
            P(),
            P("expert", None, "hid"),
            P("expert", "hid", None),
        ),
        out_specs=P(("dp", "expert", "hid"), None, None),
        check_vma=False,
    )
```

```python
import jax
import jax.numpy as jnp
from jax import lax
from jax.experimental import pallas as pl
from jax.experimental.pallas import tpu as pltpu
from jax.sharding import PartitionSpec as P

SLOTS = 2
RUN = 8


def in_hbm(value):
    return pltpu.with_memory_space_constraint(value, pltpu.HBM)


def route(images_ref, keys_ref, slots_ref, combine_ref):
    keys = keys_ref[...].astype(jnp.float32)
    unit_keys = (keys * lax.rsqrt(jnp.sum(keys * keys, axis=0, keepdims=True) + 1e-06)).astype(
        jnp.bfloat16
    )
    tokens = images_ref[...]
    floats = tokens.astype(jnp.float32)
    normed = (floats * lax.rsqrt(jnp.mean(floats * floats, axis=1, keepdims=True) + 1e-06)).astype(
        jnp.bfloat16
    )
    powers = jnp.exp(2.0 * jnp.dot(normed, unit_keys, preferred_element_type=jnp.float32))
    dispatch = (powers / jnp.sum(powers, axis=0, keepdims=True)).astype(jnp.bfloat16)
    combine_ref[...] = (powers / jnp.sum(powers, axis=1, keepdims=True)).astype(jnp.bfloat16)
    slots_ref[...] = lax.dot_general(
        dispatch, tokens, (((0,), (0,)), ((), ())), preferred_element_type=jnp.float32
    ).astype(jnp.bfloat16)


def router(tokens, slot_keys):
    (rows, width), columns = tokens.shape, slot_keys.shape[1]
    return pl.pallas_call(
        route,
        out_shape=(
            jax.ShapeDtypeStruct((columns, width), jnp.bfloat16),
            jax.ShapeDtypeStruct((rows, columns), jnp.bfloat16),
        ),
        compiler_params=pltpu.CompilerParams(vmem_limit_bytes=16 << 20),
    )(in_hbm(tokens), in_hbm(slot_keys))


def onward(value):
    groups, ring = lax.axis_size("dp"), lax.axis_size("hid")
    pairs = []
    for group in range(groups):
        step = 1 if group % 2 == 0 else ring - 1
        pairs += [(group * ring + i, group * ring + (i + step) % ring) for i in range(ring)]
    return lax.ppermute(value, ("dp", "hid"), pairs)


def to_owners(value):
    groups, owners, ring = (lax.axis_size(name) for name in ("dp", "expert", "hid"))
    teams = [
        [
            (group * owners + owner) * ring
            + (member + (group % 2 == 1 and owner % RUN < RUN // 2)) % ring
            for owner in range(owners)
        ]
        for group in range(groups)
        for member in range(ring)
    ]
    return lax.all_to_all(
        value, ("dp", "expert", "hid"), 0, 0, axis_index_groups=teams, tiled=True
    )


def expert(rows, w_in, w_out):
    hidden = jax.nn.gelu(
        jnp.dot(rows, w_in, preferred_element_type=jnp.float32), approximate=True
    ).astype(jnp.bfloat16)
    return jnp.dot(hidden, w_out, preferred_element_type=jnp.float32)


def rings(owns, w_in, w_out):
    count, stops, chunks = owns[0].shape[0], lax.axis_size("hid"), range(len(owns))
    blocks = [onward(owns[c]) for c in chunks]
    totals = [expert(blocks[c], w_in[c], w_out[c]).astype(jnp.bfloat16) for c in chunks]
    for step in range(2, stops):
        for c in chunks:
            both = onward(jnp.concatenate([blocks[c], totals[c]]))
            if step == stops - 1 and c > 0:
                both, _ = lax.optimization_barrier((both, totals[c - 1]))
            blocks[c], total = both[:count], both[count:].astype(jnp.float32)
            if step < stops - 1:
                totals[c] = (expert(blocks[c], w_in[c], w_out[c]) + total).astype(jnp.bfloat16)
            else:
                last = expert(jnp.concatenate([blocks[c], owns[c]]), w_in[c], w_out[c])
                totals[c] = (last[:count] + total).astype(jnp.bfloat16)
                blocks[c] = last[count:]
    totals = [onward(totals[c]).astype(jnp.float32) for c in chunks]
    return [(blocks[c] + totals[c]).astype(jnp.bfloat16) for c in chunks]


def layer(images_in, slot_keys, w_in, w_out):
    slot_in, combine = router(images_in[0], slot_keys)
    owners = lax.axis_size("expert")
    local_experts = w_in.shape[0]
    d_width = w_in.shape[1]
    grouped = slot_in.reshape(owners, local_experts, SLOTS, d_width)
    arrived = to_owners(grouped)
    owns = [arrived[:, b].reshape(-1, d_width) for b in range(local_experts)]
    results = [total.reshape(owners, SLOTS, d_width) for total in rings(owns, w_in, w_out)]
    results = to_owners(jnp.stack(results, axis=1))
    results = results.reshape(-1, d_width)
    mixed = jnp.dot(combine, results, preferred_element_type=jnp.float32)
    return mixed.astype(jnp.bfloat16)[None]


def solution(mesh):
    return jax.shard_map(
        layer,
        mesh=mesh,
        in_specs=(
            P(("dp", "expert", "hid"), None, None),
            P(),
            P("expert", None, "hid"),
            P("expert", "hid", None),
        ),
        out_specs=P(("dp", "expert", "hid"), None, None),
        check_vma=False,
    )
```
